1024 devices in a mesh: dp: 16 (over x, core), expert: 64 (over z, y).
Axes of the slice: x: 8, y: 8, z: 8, core: 2. Of those that a mesh axis runs over, the one named last changes fastest.
Arguments:
- hidden: bfloat16 [12288, 8, 2048], P('expert', None, 'dp'), may hold values from -6 to 6
- routing: int32 [12288, 8], P('expert'), may hold values from 0 to 63, all different within a row; in each aligned block of 192 rows (0 to 191, 192 to 383, ...) at most 30 rows name the same one
- gate_values: float32 [12288, 8], P('expert'), may hold values from 0.05 to 0.35
- out_grad: bfloat16 [12288, 4096], P('expert', 'dp'), may hold values from -6 to 6
- down_weight: bfloat16 [64, 2048, 4096], P('expert', None, 'dp'), may hold values from -0.125 to 0.125
Outputs:
- output: bfloat16 [12288, 4096], P('expert', 'dp')
- weight_grad: bfloat16 [64, 2048, 4096], P('expert', None, 'dp')
The draws below stay inside these ranges and needn't reach their ends.
Inputs may be any that keep to these rules, and one draw needn't show every extreme that they name: `routing`: each token names 8 different experts; among the tokens of one index of expert no expert is named more than 30 times.
All inputs are finite; a program needn't handle non-finite values.
Results may differ from the reference program's by a relative error of at most 0.0049.
Values may be sent and summed in bfloat16 or wider, within the bound.
No kernel may reach another device: no remote copies, remote signals or barrier semaphores. Data moves between devices by JAX's collectives and lax.ppermute only.
A program may use at most 32 MiB of HBM per device.

```python
import math
import jax
import jax.numpy as jnp
import numpy as np
from jax import lax

D = 4096
FF = 2048
TOP = 8
TOK_DEV = 192
EXPERTS = 64
CAPD = 30
TOKENS = 12288
N_EXPERT = 64


def shard_levels(rng, extent, pieces, low, high):
    factor_of = 1.0
    for position, blocks in pieces:
        draws = jax.random.uniform(jax.random.fold_in(jax.random.fold_in(rng, 6), position), (blocks,), jnp.float32, low / len(pieces), high / len(pieces))
        factor_of = factor_of * jnp.repeat(jnp.exp(draws), extent[position] // blocks).reshape((-1,) + (1,) * (len(extent) - 1 - position))
    return factor_of


def assign_block(key, own, number, rows, count, top, most, skew):
    order = jax.random.permutation(key, count)
    crowded, ordinary = load_shares(count, rows * top, most, skew, True), load_shares(count, rows * top, most, skew, False)
    places = jnp.arange(count)

    def named(tallies, rotation):
        used = int((tallies > 0).sum())
        fixed = max(1, used // 4)
        moved = fixed + (places - fixed + rotation * (used - fixed)) % max(1, count - fixed)
        return jnp.zeros((count,), jnp.int32).at[order[jnp.where(places < fixed, places, moved)]].set(jnp.asarray(tallies, jnp.int32))

    tallies = jnp.where(number % 4 == 0, named(crowded, number // 4), named(ordinary, number - number // 4 - 1))
    mixed = jax.random.permutation(jax.random.fold_in(own, 3), count)
    giver, sink = mixed[0:count // 2 * 2:2], mixed[1:count // 2 * 2:2]
    room = jnp.minimum(tallies[giver] - 1, most - tallies[sink]) // 2
    room = jnp.where((giver == order[0]) | (sink == order[0]) | (tallies[sink] == 0), 0, jnp.maximum(room, 0))
    moved = jax.random.randint(jax.random.fold_in(own, 4), (count // 2,), 0, 1 << 20) % (room + 1)
    tallies = tallies.at[giver].add(-moved).at[sink].add(moved)
    labels = jnp.searchsorted(jnp.cumsum(tallies), jnp.arange(rows * top), side="right").astype(jnp.int32)
    grid = labels.reshape(top, rows).T
    grid = grid[jax.random.permutation(jax.random.fold_in(own, 1), rows)]
    rotation = jax.random.randint(jax.random.fold_in(own, 2), (rows, 1), 0, top)
    return jnp.take_along_axis(grid, (jnp.arange(top)[None, :] + rotation) % top, axis=1)


def load_shares(count, total, reach, skew, full):
    loads = [(1 << 20) // math.isqrt(grade ** skew) + 1 for grade in range(1, count + 1)]
    largest = reach if full else min(reach, max(-(-total // count), total * loads[0] // sum(loads)))
    least = 1 if total - largest >= count - 1 else 0
    holding, rest = [largest] + [least] * (count - 1), total - largest - least * (count - 1)
    while rest > 0:
        candidates = [i for i in range(1, count) if holding[i] < largest] or [i for i in range(1, count) if holding[i] < reach]
        mass, remaining = sum([loads[i] for i in candidates]), rest
        for i in candidates:
            addition = min(reach - holding[i], max(1, remaining * loads[i] // mass), rest)
            holding[i] = holding[i] + addition
            rest = rest - addition
    return np.array(holding)


def centred(stream_key, dims, width, limit, cuts=(), kind=jnp.bfloat16):
    gain = shard_levels(stream_key, dims, cuts, -0.22, 0.18) if cuts else 1.0
    array = jax.random.normal(stream_key, dims, jnp.float32) * width * gain
    return jnp.minimum(jnp.maximum(array, -limit), limit).astype(kind)


def setup_inputs(seed: int = 0) -> dict:
    arg_keys = jax.random.split(jax.random.key(seed), 6)
    hidden = centred(arg_keys[0], (TOKENS, TOP, FF), 1.0, 6.0, ((0, 64), (2, 16)))
    routing_keys = jax.random.split(jax.random.fold_in(arg_keys[1], 1), TOKENS // TOK_DEV)
    routing_turns = jax.random.permutation(jax.random.fold_in(arg_keys[1], 3), TOKENS // TOK_DEV)
    routing = jax.vmap(lambda own, number: assign_block(jax.random.fold_in(arg_keys[1], 2), own, number, TOK_DEV, EXPERTS, TOP, CAPD, 2))(routing_keys, routing_turns).reshape((TOKENS, TOP))
    gate_values = jnp.clip(0.05 + 0.29999999 * jax.random.uniform(arg_keys[2], (TOKENS, TOP), jnp.float32) ** shard_levels(arg_keys[2], (TOKENS, TOP), ((0, 64),), -0.2, 0.2), 0.05, 0.35)
    out_grad = centred(arg_keys[3], (TOKENS, D), 1.0, 6.0, ((0, 64), (1, 16)))
    down_weight = centred(arg_keys[4], (EXPERTS, FF, D), FF ** -0.5, 0.125, ((0, 64), (2, 16)))
    return dict(hidden=hidden, routing=routing, gate_values=gate_values, out_grad=out_grad, down_weight=down_weight)


def reference(hidden, routing, gate_values, out_grad, down_weight):
    slot_count = TOKENS * TOP
    max_rows = N_EXPERT * CAPD
    flat_route = routing.reshape(slot_count).astype(jnp.int32)
    sorted_slots = jnp.argsort(flat_route, stable=True).astype(jnp.int32)
    sorted_slots = jnp.concatenate([sorted_slots, jnp.zeros((max_rows,), jnp.int32)])
    counts = jax.ops.segment_sum(jnp.ones((slot_count,), jnp.int32), flat_route, num_segments=EXPERTS).astype(jnp.int32)
    offsets = (jnp.cumsum(counts) - counts).astype(jnp.int32)
    hidden_flat = hidden.reshape(slot_count, FF)
    gate_flat = gate_values.reshape(slot_count)

    def one_expert(out_sum, inputs):
        weight, begin_at, live_count = inputs
        slot_ids = lax.dynamic_slice_in_dim(sorted_slots, begin_at, max_rows)
        is_live = jnp.arange(max_rows, dtype=jnp.int32) < live_count
        picked = jnp.where(is_live[:, None], hidden_flat[slot_ids], jnp.zeros((), hidden.dtype))
        token_idx = (slot_ids // TOP).astype(jnp.int32)
        gate_rows = jnp.where(is_live, gate_flat[slot_ids], jnp.zeros((), gate_values.dtype))
        scaled = (gate_rows[:, None] * out_grad[token_idx].astype(jnp.float32)).astype(jnp.bfloat16)
        expert_out = jnp.dot(picked, weight, preferred_element_type=jnp.float32).astype(jnp.bfloat16)
        out_sum = out_sum.at[token_idx].add(gate_rows[:, None] * expert_out.astype(jnp.float32))
        expert_grad = lax.dot_general(picked, scaled, (((0,), (0,)), ((), ())), preferred_element_type=jnp.float32)
        return out_sum, expert_grad.astype(jnp.bfloat16)

    zero_sum = jnp.zeros((TOKENS, D), jnp.float32)
    out_sum, expert_grads = lax.scan(one_expert, zero_sum, (down_weight, offsets, counts))
    return out_sum.astype(jnp.bfloat16), expert_grads
```

```python
import functools

import jax
import jax.numpy as jnp
from jax import lax
from jax.experimental import pallas as pl
from jax.experimental.pallas import tpu as pltpu
from jax.sharding import PartitionSpec as P


BF, F32, I32 = jnp.bfloat16, jnp.float32, jnp.int32
PITCH = 32
PER = 8
VMEM = pl.BlockSpec(memory_space=pltpu.VMEM)
SMEM = pl.BlockSpec(memory_space=pltpu.SMEM)


def iota(shape, dim):
    return lax.broadcasted_iota(I32, shape, dim)


def cost(flops, nbytes):
    return pl.CostEstimate(flops=flops, bytes_accessed=nbytes, transcendentals=0)


def ranks(route, n_exp):
    top, tokens = route.shape
    experts = iota((n_exp, tokens), 0)
    named = jnp.zeros((n_exp, tokens), F32)
    for k in range(top):
        named += (route[k : k + 1, :] == experts).astype(F32)
    before = (iota((tokens, tokens), 0) < iota((tokens, tokens), 1)).astype(F32).astype(BF)
    place = jnp.dot(named.astype(BF), before, preferred_element_type=F32)
    return named, place, experts


def slot_rows(route, n_exp):
    top, tokens = route.shape
    _, place, experts = ranks(route, n_exp)
    rank = jnp.concatenate(
        [
            jnp.sum(jnp.where(route[k : k + 1, :] == experts, place, 0.0), axis=0, keepdims=True)
            for k in range(top)
        ],
        axis=0,
    )
    slots = tokens * top
    spread = (iota((tokens, slots), 1) // top == iota((tokens, slots), 0)).astype(F32).astype(BF)
    rank_s = jnp.dot(rank.astype(BF), spread, preferred_element_type=F32)
    route_s = jnp.dot(route.astype(F32).astype(BF), spread, preferred_element_type=F32)
    mine = iota((top, slots), 1) % top == iota((top, slots), 0)
    row = jnp.sum(jnp.where(mine, route_s * PITCH + rank_s, 0.0), axis=0, keepdims=True)
    return row.astype(I32)


def send_hidden_kernel(n_exp, cap, route_ref, hidden_ref, out_ref):
    row = slot_rows(route_ref[...], n_exp)
    hidden = hidden_ref[...]
    slots = row.shape[1]

    def step(g, _):
        here = iota((PER * PITCH, slots), 0) + g * (PER * PITCH)
        hot = (here == row).astype(F32).astype(BF)
        rows = jnp.dot(hot, hidden, preferred_element_type=F32).astype(BF)
        for j in range(PER):
            out_ref[g * PER + j] = rows[j * PITCH : j * PITCH + cap]
        return 0

    lax.fori_loop(0, n_exp // PER, step, 0)


def send_hidden(route_t, hidden_rows, n_exp, cap):
    slots, part = hidden_rows.shape
    return pl.pallas_call(
        functools.partial(send_hidden_kernel, n_exp, cap),
        out_shape=jax.ShapeDtypeStruct((n_exp, cap, part), BF),
        in_specs=[VMEM, VMEM],
        out_specs=VMEM,
        compiler_params=pltpu.CompilerParams(vmem_limit_bytes=12 << 20),
        cost_estimate=cost(2 * n_exp * PITCH * slots * part, 1 << 20),
        name="send_hidden",
    )(route_t, hidden_rows)


def token_tables(route, gate, n_exp):
    named, place, experts = ranks(route, n_exp)
    gates = jnp.zeros(place.shape, F32)
    for k in range(route.shape[0]):
        gates = jnp.where(route[k : k + 1, :] == experts, gate[k : k + 1, :], gates)
    return jnp.where(named > 0.5, place, -1.0), gates


def send_grads_kernel(n_exp, route_ref, gate_ref, grad_ref, out_ref, place_ref, gates_ref):
    place, gates = token_tables(route_ref[...], gate_ref[...], n_exp)
    place_ref[...] = place.astype(I32)
    gates_ref[...] = gates
    grad = grad_ref[...]
    tokens = grad.shape[0]

    def step(g, _):
        at = pl.ds(pl.multiple_of(g * PER, PER), PER)
        spot, value = place_ref[at, :], gates_ref[at, :]
        slot = iota((PITCH, tokens), 0)
        hots, scales = [], []
        for j in range(PER):
            hot = spot[j : j + 1, :] == slot
            hots.append(hot.astype(F32).astype(BF))
            scales.append(jnp.sum(jnp.where(hot, value[j : j + 1, :], 0.0), axis=1, keepdims=True))
        rows = jnp.dot(jnp.concatenate(hots, axis=0), grad, preferred_element_type=F32)
        to = pl.ds(pl.multiple_of(g * (PER * PITCH), PER * PITCH), PER * PITCH)
        out_ref[to, :] = (jnp.concatenate(scales, axis=0) * rows).astype(BF)
        return 0

    lax.fori_loop(0, n_exp // PER, step, 0)


def send_grads(route_t, gate_t, grad, n_exp):
    tokens, part = grad.shape
    return pl.pallas_call(
        functools.partial(send_grads_kernel, n_exp),
        out_shape=jax.ShapeDtypeStruct((n_exp * PITCH, part), BF),
        in_specs=[VMEM] * 3,
        out_specs=VMEM,
        scratch_shapes=[pltpu.VMEM((n_exp, tokens), I32), pltpu.VMEM((n_exp, tokens), F32)],
        compiler_params=pltpu.CompilerParams(vmem_limit_bytes=12 << 20),
        cost_estimate=cost(2 * n_exp * PITCH * tokens * part, 1 << 20),
        name="send_grads",
    )(route_t, gate_t, grad)


def padded(block):
    fill = jnp.zeros((PITCH - block.shape[1], block.shape[2]), block.dtype)
    pieces = []
    for j in range(block.shape[0]):
        pieces += [block[j], fill]
    return jnp.concatenate(pieces, axis=0)


WIDE = 16


def early_kernel(index_ref, *refs):
    *blocks, own_ref, other_ref, keep_ref, send_ref, w_ref = refs
    n_exp, _, part = blocks[0].shape
    width = own_ref.shape[1]
    for j in range(len(blocks)):
        at = pl.ds(pl.multiple_of(index_ref[j] * part, part), part)
        w_ref[j * part : (j + 1) * part, :width] = own_ref[at, :]
        w_ref[j * part : (j + 1) * part, width:] = other_ref[at, :]

    def step(g, _):
        at = pl.ds(pl.multiple_of(g * WIDE, WIDE), WIDE)
        to = pl.ds(pl.multiple_of(g * (WIDE * PITCH), WIDE * PITCH), WIDE * PITCH)
        left = jnp.concatenate([padded(b[at]) for b in blocks], axis=1)
        rows = jnp.dot(left, w_ref[...], preferred_element_type=F32)
        keep_ref[to, :] = rows[:, :width]
        send_ref[to, :] = rows[:, width:].astype(BF)
        return 0

    lax.fori_loop(0, n_exp // WIDE, step, 0)


def early_product(index, blocks, own_w, other_w):
    n_exp, _, part = blocks[0].shape
    width = own_w.shape[1]
    count = len(blocks)
    return pl.pallas_call(
        early_kernel,
        out_shape=(
            jax.ShapeDtypeStruct((n_exp * PITCH, width), F32),
            jax.ShapeDtypeStruct((n_exp * PITCH, width), BF),
        ),
        in_specs=[SMEM] + [VMEM] * (count + 2),
        out_specs=(VMEM, VMEM),
        scratch_shapes=[pltpu.VMEM((count * part, 2 * width), BF)],
        compiler_params=pltpu.CompilerParams(vmem_limit_bytes=28 << 20),
        cost_estimate=cost(4 * n_exp * PITCH * count * part * width, 8 << 20),
        name="early_product",
    )(index, *blocks, own_w, other_w)


def late_kernel(index_ref, a_ref, b_ref, other_a_ref, other_b_ref, w_ref, keep_ref, got_ref, out_ref):
    half, cap, part = a_ref.shape
    own = w_ref[pl.ds(pl.multiple_of(index_ref[0] * part, part), part), :]
    other = w_ref[pl.ds(pl.multiple_of(index_ref[1] * part, part), part), :]
    w = jnp.concatenate([own, other], axis=0)
    for h, (mine, theirs) in enumerate(((a_ref, other_a_ref), (b_ref, other_b_ref))):

        def step(g, _, h=h, mine=mine, theirs=theirs):
            at = pl.ds(pl.multiple_of(g * PER, PER), PER)
            first = h * half * PITCH
            frm = pl.ds(pl.multiple_of(first + g * (PER * PITCH), PER * PITCH), PER * PITCH)
            left = jnp.concatenate([padded(mine[at]), padded(theirs[at])], axis=1)
            rows = jnp.dot(left, w, preferred_element_type=F32)
            rows = (rows + keep_ref[frm, :] + got_ref[frm, :].astype(F32)).astype(BF)
            for j in range(PER):
                out_ref[h * half + g * PER + j] = rows[j * PITCH : j * PITCH + cap]
            return 0

        lax.fori_loop(0, half // PER, step, 0)


def late_product(index, a, b, other_a, other_b, own_w, keep, got):
    half, cap, part = a.shape
    width = own_w.shape[1]
    return pl.pallas_call(
        late_kernel,
        out_shape=jax.ShapeDtypeStruct((2 * half, cap, width), BF),
        in_specs=[SMEM] + [VMEM] * 7,
        out_specs=VMEM,
        compiler_params=pltpu.CompilerParams(vmem_limit_bytes=20 << 20),
        cost_estimate=cost(8 * half * PITCH * part * width, 6 << 20),
        name="late_product",
    )(index, a, b, other_a, other_b, own_w, keep, got)


def grad_kernel(index_ref, *refs):
    *blocks, last_a, last_b, own_ref, other_ref, keep_ref, send_ref = refs
    n_exp, _, part = blocks[0].shape
    width = own_ref.shape[1]
    chunk = n_exp // 2
    for j in range(len(blocks) + 1):
        total = jnp.zeros((part, 2 * width), F32)
        for i in range(2):
            block = blocks[j][i * chunk : (i + 1) * chunk] if j < len(blocks) else (last_a, last_b)[i][...]
            rows = slice(i * chunk * PITCH, (i + 1) * chunk * PITCH)
            right = jnp.concatenate([own_ref[rows, :], other_ref[rows, :]], axis=1)
            total += lax.dot_general(
                padded(block), right, (((0,), (0,)), ((), ())), preferred_element_type=F32
            )
        at = index_ref[j] // 2
        keep_ref[at] = total[:, :width].astype(BF)
        send_ref[at] = total[:, width:].astype(BF)


def half_grad(index, blocks, last_a, last_b, own_g, other_g):
    rows, width = own_g.shape
    part = blocks[0].shape[2]
    count = len(blocks) + 1
    shape = jax.ShapeDtypeStruct((count, part, width), BF)
    return pl.pallas_call(
        grad_kernel,
        out_shape=(shape, shape),
        in_specs=[SMEM] + [VMEM] * (len(blocks) + 4),
        out_specs=(VMEM, VMEM),
        compiler_params=pltpu.CompilerParams(vmem_limit_bytes=28 << 20),
        cost_estimate=cost(4 * rows * count * part * width, 8 << 20),
        name="half_grad",
    )(index, *blocks, last_a, last_b, own_g, other_g)


def combine_kernel(n_exp, route_ref, gate_ref, got_ref, out_ref):
    place, gates = token_tables(route_ref[...], gate_ref[...], n_exp)
    spots, gates = place.T, gates.T
    tokens = spots.shape[0]
    lanes = PER * PITCH
    high = gates.astype(BF)
    rest = gates - high.astype(F32)
    mid = rest.astype(BF)
    low = (rest - mid.astype(F32)).astype(BF)
    table = jnp.concatenate([spots.astype(BF), high, mid, low], axis=0)
    slot = iota((tokens, lanes), 1) % PITCH
    total = jnp.zeros((tokens, out_ref.shape[1]), F32)
    for g in range(n_exp // PER):
        spread = (iota((n_exp, lanes), 1) // PITCH + g * PER == iota((n_exp, lanes), 0)).astype(F32).astype(BF)
        wide = jnp.dot(table, spread, preferred_element_type=F32)
        here = wide[:tokens] == slot.astype(F32)
        got = padded(got_ref[g * PER : (g + 1) * PER])
        for p in range(1, 4):
            weight = jnp.where(here, wide[p * tokens : (p + 1) * tokens], 0.0).astype(BF)
            total += jnp.dot(weight, got, preferred_element_type=F32)
    out_ref[...] = total.astype(BF)


def combine(route_t, gate_t, got):
    n_exp, _, width = got.shape
    tokens = route_t.shape[1]
    return pl.pallas_call(
        functools.partial(combine_kernel, n_exp),
        out_shape=jax.ShapeDtypeStruct((tokens, width), BF),
        in_specs=[VMEM] * 3,
        out_specs=VMEM,
        compiler_params=pltpu.CompilerParams(vmem_limit_bytes=12 << 20),
        cost_estimate=cost(8 * tokens * n_exp * PITCH * width, 1 << 20),
        name="combine",
    )(route_t, gate_t, got)


def body(hidden, routing, gate_values, out_grad, down_weight):
    n_exp = lax.axis_size("expert")
    n_dp = lax.axis_size("dp")
    tokens, top, part = hidden.shape
    width = out_grad.shape[1]
    cap = min(tokens, max(2, tokens * top // n_exp + tokens * top // (4 * n_exp)))
    me = lax.axis_index("dp")
    core = me % 2
    n_x = n_dp // 2
    place = me // 2

    def shift(value, by):
        return lax.ppermute(value, "dp", [(i, (i + 2 * by) % n_dp) for i in range(n_dp)])

    def swap(value):
        return lax.ppermute(value, "dp", [(i, i ^ 1) for i in range(n_dp)])

    def exchange(value):
        return lax.all_to_all(value, "expert", split_axis=0, concat_axis=0, tiled=True)

    route_t = routing.T
    gate_t = gate_values.T
    weight = down_weight[0]
    mine = exchange(send_hidden(route_t, hidden.reshape(tokens * top, part), n_exp, cap))
    grads = send_grads(route_t, gate_t, out_grad, n_exp).reshape(n_exp, PITCH, width)
    grads = exchange(grads).reshape(n_exp * PITCH, width)
    other_weight = swap(weight)
    up = down = mine
    blocks, offsets = [mine], [0]
    for step in range(1, n_x // 2):
        up, down = shift(up, 1), shift(down, -1)
        blocks += [up, down]
        offsets += [-step, step]
    half = n_exp // 2
    last_a, last_b = shift(up[:half], 1), shift(down[half:], -1)
    far = 2 * ((place + n_x // 2) % n_x)
    index = jnp.stack([2 * ((place + o) % n_x) + core for o in offsets] + [far + core]).astype(I32)
    far_index = jnp.stack([far + core, far + 1 - core]).astype(I32)
    other_grads = swap(grads)

    keep, send = early_product(index, blocks, weight, other_weight)
    got = swap(send)
    other_a, other_b = swap(last_a), swap(last_b)
    rows = late_product(far_index, last_a, last_b, other_a, other_b, weight, keep, got)
    returned = exchange(rows)
    keep_g, send_g = half_grad(index, blocks, last_a, last_b, grads, other_grads)
    got_g = swap(send_g)
    first = jnp.where(core == 0, keep_g, got_g)
    second = jnp.where(core == 0, got_g, keep_g)
    weight_grad = jnp.stack([first, second], axis=1).reshape(1, n_dp * part, width)
    output = combine(route_t, gate_t, returned)
    return output, weight_grad


def solution(mesh):
    placed = (
        P("expert", None, "dp"),
        P("expert", None),
        P("expert", None),
        P("expert", "dp"),
        P("expert", None, "dp"),
    )

    return jax.shard_map(
        body,
        mesh=mesh,
        in_specs=placed,
        out_specs=(P("expert", "dp"), P("expert", None, "dp")),
        check_vma=False,
    )
```

```python
import functools

import jax
import jax.numpy as jnp
from jax import lax
from jax.experimental import pallas as pl
from jax.experimental.pallas import tpu as pltpu
from jax.sharding import PartitionSpec as P


BF, F32, I32 = jnp.bfloat16, jnp.float32, jnp.int32
PITCH = 32
PER = 8
VMEM = pl.BlockSpec(memory_space=pltpu.VMEM)
SMEM = pl.BlockSpec(memory_space=pltpu.SMEM)


def iota(shape, dim):
    return lax.broadcasted_iota(I32, shape, dim)


def cost(flops, nbytes):
    return pl.CostEstimate(flops=flops, bytes_accessed=nbytes, transcendentals=0)


def ranks(route, n_exp):
    top, tokens = route.shape
    experts = iota((n_exp, tokens), 0)
    named = jnp.zeros((n_exp, tokens), F32)
    for k in range(top):
        named += (route[k : k + 1, :] == experts).astype(F32)
    before = (iota((tokens, tokens), 0) < iota((tokens, tokens), 1)).astype(F32).astype(BF)
    place = jnp.dot(named.astype(BF), before, preferred_element_type=F32)
    return named, place, experts


def slot_rows(route, n_exp):
    top, tokens = route.shape
    _, place, experts = ranks(route, n_exp)
    rank = jnp.concatenate(
        [
            jnp.sum(jnp.where(route[k : k + 1, :] == experts, place, 0.0), axis=0, keepdims=True)
            for k in range(top)
        ],
        axis=0,
    )
    slots = tokens * top
    spread = (iota((tokens, slots), 1) // top == iota((tokens, slots), 0)).astype(F32).astype(BF)
    rank_s = jnp.dot(rank.astype(BF), spread, preferred_element_type=F32)
    route_s = jnp.dot(route.astype(F32).astype(BF), spread, preferred_element_type=F32)
    mine = iota((top, slots), 1) % top == iota((top, slots), 0)
    row = jnp.sum(jnp.where(mine, route_s * PITCH + rank_s, 0.0), axis=0, keepdims=True)
    return row.astype(I32)


def send_hidden_kernel(n_exp, cap, route_ref, hidden_ref, out_ref):
    row = slot_rows(route_ref[...], n_exp)
    hidden = hidden_ref[...]
    slots = row.shape[1]

    def step(g, _):
        here = iota((PER * PITCH, slots), 0) + g * (PER * PITCH)
        hot = (here == row).astype(F32).astype(BF)
        rows = jnp.dot(hot, hidden, preferred_element_type=F32).astype(BF)
        for j in range(PER):
            out_ref[g * PER + j] = rows[j * PITCH : j * PITCH + cap]
        return 0

    lax.fori_loop(0, n_exp // PER, step, 0)


def send_hidden(route_t, hidden_rows, n_exp, cap):
    slots, part = hidden_rows.shape
    return pl.pallas_call(
        functools.partial(send_hidden_kernel, n_exp, cap),
        out_shape=jax.ShapeDtypeStruct((n_exp, cap, part), BF),
        in_specs=[VMEM, VMEM],
        out_specs=VMEM,
        compiler_params=pltpu.CompilerParams(vmem_limit_bytes=12 << 20),
        cost_estimate=cost(2 * n_exp * PITCH * slots * part, 1 << 20),
        name="send_hidden",
    )(route_t, hidden_rows)


def token_tables(route, gate, n_exp):
    named, place, experts = ranks(route, n_exp)
    gates = jnp.zeros(place.shape, F32)
    for k in range(route.shape[0]):
        gates = jnp.where(route[k : k + 1, :] == experts, gate[k : k + 1, :], gates)
    return jnp.where(named > 0.5, place, -1.0), gates


def send_grads_kernel(n_exp, route_ref, gate_ref, grad_ref, out_ref, place_ref, gates_ref):
    place, gates = token_tables(route_ref[...], gate_ref[...], n_exp)
    place_ref[...] = place.astype(I32)
    gates_ref[...] = gates
    grad = grad_ref[...]
    tokens = grad.shape[0]

    def step(g, _):
        at = pl.ds(pl.multiple_of(g * PER, PER), PER)
        spot, value = place_ref[at, :], gates_ref[at, :]
        slot = iota((PITCH, tokens), 0)
        hots, scales = [], []
        for j in range(PER):
            hot = spot[j : j + 1, :] == slot
            hots.append(hot.astype(F32).astype(BF))
            scales.append(jnp.sum(jnp.where(hot, value[j : j + 1, :], 0.0), axis=1, keepdims=True))
        rows = jnp.dot(jnp.concatenate(hots, axis=0), grad, preferred_element_type=F32)
        to = pl.ds(pl.multiple_of(g * (PER * PITCH), PER * PITCH), PER * PITCH)
        out_ref[to, :] = (jnp.concatenate(scales, axis=0) * rows).astype(BF)
        return 0

    lax.fori_loop(0, n_exp // PER, step, 0)


def send_grads(route_t, gate_t, grad, n_exp):
    tokens, part = grad.shape
    return pl.pallas_call(
        functools.partial(send_grads_kernel, n_exp),
        out_shape=jax.ShapeDtypeStruct((n_exp * PITCH, part), BF),
        in_specs=[VMEM] * 3,
        out_specs=VMEM,
        scratch_shapes=[pltpu.VMEM((n_exp, tokens), I32), pltpu.VMEM((n_exp, tokens), F32)],
        compiler_params=pltpu.CompilerParams(vmem_limit_bytes=12 << 20),
        cost_estimate=cost(2 * n_exp * PITCH * tokens * part, 1 << 20),
        name="send_grads",
    )(route_t, gate_t, grad)


def padded(block):
    fill = jnp.zeros((PITCH - block.shape[1], block.shape[2]), block.dtype)
    pieces = []
    for j in range(block.shape[0]):
        pieces += [block[j], fill]
    return jnp.concatenate(pieces, axis=0)


WIDE = 16


def early_kernel(index_ref, *refs):
    *blocks, own_ref, other_ref, keep_ref, send_ref, w_ref = refs
    n_exp, _, part = blocks[0].shape
    width = own_ref.shape[1]
    for j in range(len(blocks)):
        at = pl.ds(pl.multiple_of(index_ref[j] * part, part), part)
        w_ref[j * part : (j + 1) * part, :width] = own_ref[at, :]
        w_ref[j * part : (j + 1) * part, width:] = other_ref[at, :]

    def step(g, _):
        at = pl.ds(pl.multiple_of(g * WIDE, WIDE), WIDE)
        to = pl.ds(pl.multiple_of(g * (WIDE * PITCH), WIDE * PITCH), WIDE * PITCH)
        left = jnp.concatenate([padded(b[at]) for b in blocks], axis=1)
        rows = jnp.dot(left, w_ref[...], preferred_element_type=F32)
        keep_ref[to, :] = rows[:, :width]
        send_ref[to, :] = rows[:, width:].astype(BF)
        return 0

    lax.fori_loop(0, n_exp // WIDE, step, 0)


def early_product(index, blocks, own_w, other_w):
    n_exp, _, part = blocks[0].shape
    width = own_w.shape[1]
    count = len(blocks)
    return pl.pallas_call(
        early_kernel,
        out_shape=(
            jax.ShapeDtypeStruct((n_exp * PITCH, width), F32),
            jax.ShapeDtypeStruct((n_exp * PITCH, width), BF),
        ),
        in_specs=[SMEM] + [VMEM] * (count + 2),
        out_specs=(VMEM, VMEM),
        scratch_shapes=[pltpu.VMEM((count * part, 2 * width), BF)],
        cost_estimate=cost(4 * n_exp * PITCH * count * part * width, 8 << 20),
        name="early_product",
    )(index, *blocks, own_w, other_w)


def late_kernel(own, other, index_ref, mine_ref, theirs_ref, w_ref, keep_ref, got_ref, out_ref):
    n_exp, cap, part = mine_ref.shape
    first = w_ref[pl.ds(pl.multiple_of(index_ref[own] * part, part), part), :]
    second = w_ref[pl.ds(pl.multiple_of(index_ref[other] * part, part), part), :]
    w = jnp.concatenate([first, second], axis=0)

    def step(g, _):
        at = pl.ds(pl.multiple_of(g * WIDE, WIDE), WIDE)
        frm = pl.ds(pl.multiple_of(g * (WIDE * PITCH), WIDE * PITCH), WIDE * PITCH)
        left = jnp.concatenate([padded(mine_ref[at]), padded(theirs_ref[at])], axis=1)
        rows = jnp.dot(left, w, preferred_element_type=F32)
        rows = (rows + keep_ref[frm, :] + got_ref[frm, :].astype(F32)).astype(BF)
        for j in range(WIDE):
            out_ref[g * WIDE + j] = rows[j * PITCH : j * PITCH + cap]
        return 0

    lax.fori_loop(0, n_exp // WIDE, step, 0)


def late_product(own, other, index, mine, theirs, own_w, keep, got):
    n_exp, cap, part = mine.shape
    width = own_w.shape[1]
    return pl.pallas_call(
        functools.partial(late_kernel, own, other),
        out_shape=jax.ShapeDtypeStruct((n_exp, cap, width), BF),
        in_specs=[SMEM] + [VMEM] * 5,
        out_specs=VMEM,
        compiler_params=pltpu.CompilerParams(vmem_limit_bytes=20 << 20),
        cost_estimate=cost(4 * n_exp * PITCH * part * width, 6 << 20),
        name="late_product",
    )(index, mine, theirs, own_w, keep, got)


def grad_kernel(*refs):
    *blocks, own_ref, other_ref, keep_ref, send_ref = refs
    n_exp, _, part = blocks[0].shape
    width = own_ref.shape[1]
    chunk = n_exp // 2
    for j in range(len(blocks)):
        total = jnp.zeros((part, 2 * width), F32)
        for i in range(2):
            rows = slice(i * chunk * PITCH, (i + 1) * chunk * PITCH)
            left = padded(blocks[j][i * chunk : (i + 1) * chunk])
            right = jnp.concatenate([own_ref[rows, :], other_ref[rows, :]], axis=1)
            total += lax.dot_general(left, right, (((0,), (0,)), ((), ())), preferred_element_type=F32)
        keep_ref[j] = total[:, :width].astype(BF)
        send_ref[j] = total[:, width:].astype(BF)


def half_grad(blocks, own_g, other_g):
    rows, width = own_g.shape
    part = blocks[0].shape[2]
    count = len(blocks)
    shape = jax.ShapeDtypeStruct((count, part, width), BF)
    return pl.pallas_call(
        grad_kernel,
        out_shape=(shape, shape),
        in_specs=[VMEM] * (len(blocks) + 2),
        out_specs=(VMEM, VMEM),
        cost_estimate=cost(4 * rows * count * part * width, 8 << 20),
        name="half_grad",
    )(*blocks, own_g, other_g)


def merge_kernel(index_ref, keep_ref, got_ref, out_ref):
    count = keep_ref.shape[0]
    for j in range(count):
        out_ref[index_ref[j]] = keep_ref[j]
        out_ref[index_ref[count + j]] = got_ref[j]


def merge(index, keep, got):
    count, part, width = keep.shape
    return pl.pallas_call(
        merge_kernel,
        out_shape=jax.ShapeDtypeStruct((2 * count, part, width), BF),
        in_specs=[SMEM, VMEM, VMEM],
        out_specs=VMEM,
        compiler_params=pltpu.CompilerParams(vmem_limit_bytes=8 << 20),
        cost_estimate=cost(0, 4 << 20),
        name="merge",
    )(index, keep, got)


def combine_kernel(n_exp, route_ref, gate_ref, got_ref, out_ref):
    place, gates = token_tables(route_ref[...], gate_ref[...], n_exp)
    spots, gates = place.T, gates.T
    tokens = spots.shape[0]
    lanes = PER * PITCH
    high = gates.astype(BF)
    rest = gates - high.astype(F32)
    mid = rest.astype(BF)
    low = (rest - mid.astype(F32)).astype(BF)
    table = jnp.concatenate([spots.astype(BF), high, mid, low], axis=0)
    slot = iota((tokens, lanes), 1) % PITCH
    total = jnp.zeros((tokens, out_ref.shape[1]), F32)
    for g in range(n_exp // PER):
        spread = (iota((n_exp, lanes), 1) // PITCH + g * PER == iota((n_exp, lanes), 0)).astype(F32).astype(BF)
        wide = jnp.dot(table, spread, preferred_element_type=F32)
        here = wide[:tokens] == slot.astype(F32)
        got = padded(got_ref[g * PER : (g + 1) * PER])
        for p in range(1, 4):
            weight = jnp.where(here, wide[p * tokens : (p + 1) * tokens], 0.0).astype(BF)
            total += jnp.dot(weight, got, preferred_element_type=F32)
    out_ref[...] = total.astype(BF)


def combine(route_t, gate_t, got):
    n_exp, _, width = got.shape
    tokens = route_t.shape[1]
    return pl.pallas_call(
        functools.partial(combine_kernel, n_exp),
        out_shape=jax.ShapeDtypeStruct((tokens, width), BF),
        in_specs=[VMEM] * 3,
        out_specs=VMEM,
        compiler_params=pltpu.CompilerParams(vmem_limit_bytes=12 << 20),
        cost_estimate=cost(8 * tokens * n_exp * PITCH * width, 1 << 20),
        name="combine",
    )(route_t, gate_t, got)


def body(hidden, routing, gate_values, out_grad, down_weight):
    n_exp = lax.axis_size("expert")
    n_dp = lax.axis_size("dp")
    tokens, top, part = hidden.shape
    width = out_grad.shape[1]
    cap = min(tokens, max(2, tokens * top // n_exp + tokens * top // (4 * n_exp)))
    me = lax.axis_index("dp")
    core = me % 2
    n_x = n_dp // 2
    place = me // 2

    def ring(value):
        forth = [(2 * x, 2 * ((x + 1) % n_x)) for x in range(n_x)]
        back = [(2 * x + 1, 2 * ((x - 1) % n_x) + 1) for x in range(n_x)]
        return lax.ppermute(value, "dp", forth + back)

    def swap(value):
        return lax.ppermute(value, "dp", [(i, i ^ 1) for i in range(n_dp)])

    def exchange(value):
        return lax.all_to_all(value, "expert", split_axis=0, concat_axis=0, tiled=True)

    route_t = routing.T
    gate_t = gate_values.T
    weight = down_weight[0]
    mine = exchange(send_hidden(route_t, hidden.reshape(tokens * top, part), n_exp, cap))
    grads = send_grads(route_t, gate_t, out_grad, n_exp).reshape(n_exp, PITCH, width)
    grads = exchange(grads).reshape(n_exp * PITCH, width)
    other_weight = swap(weight)
    same, cross = mine, swap(mine)
    blocks, hops, flips = [mine], [0], [0]
    for step in range(1, n_x // 2):
        same, cross = ring(same), ring(cross)
        blocks += [same, cross]
        hops += [step, step]
        flips += [0, 1]
    far = ring(same)
    hops, flips = jnp.array(hops + [n_x // 2], I32), jnp.array(flips + [0], I32)
    towards = 2 * core - 1
    taken = [
        2 * ((place + way * hops + n_x) % n_x) + (parity + flips) % 2
        for way, parity in ((towards, core), (-towards, 1 - core))
    ]
    index = jnp.concatenate(taken).astype(I32)
    other_grads = swap(grads)

    keep, send = early_product(index, blocks, weight, other_weight)
    got = swap(send)
    count = len(blocks)
    rows = late_product(count, 2 * count + 1, index, far, swap(far), weight, keep, got)
    returned = exchange(rows)
    keep_g, send_g = half_grad(blocks + [far], grads, other_grads)
    got_g = swap(send_g)
    weight_grad = merge(index, keep_g, got_g).reshape(1, n_dp * part, width)
    output = combine(route_t, gate_t, returned)
    return output, weight_grad


def solution(mesh):
    placed = (
        P("expert", None, "dp"),
        P("expert", None),
        P("expert", None),
        P("expert", "dp"),
        P("expert", None, "dp"),
    )

    return jax.shard_map(
        body,
        mesh=mesh,
        in_specs=placed,
        out_specs=(P("expert", "dp"), P("expert", None, "dp")),
        check_vma=False,
    )
```
